32 devices in a mesh: seq: 8 (over z, y), view: 4 (over x, core).
Axes of the slice: x: 2, y: 2, z: 4, core: 2. Of those that a mesh axis runs over, the one named last changes fastest.
Arguments:
- ssd_input: bfloat16 [8, 4, 512, 2048], P('seq', 'view'), may hold values from -21 to 21
- gate_input: bfloat16 [8, 4, 512, 2048], P('seq', 'view'), may hold values from -6 to 6
- b_matrix: bfloat16 [8, 4, 512, 128], P('seq', 'view'), may hold values from -6 to 6
- c_matrix: bfloat16 [8, 4, 512, 128], P('seq', 'view'), may hold values from -0.52734375 to 0.52734375
- log_decay: float32 [8, 4, 32, 512], P('seq', 'view'), may hold values from -1 to 0, as said below
- d_skip: float32 [32], replicated, may hold values from 1 to 4
- norm_gain: float32 [2048], replicated, may hold values from 0.1 to 1.9
- out_weight: bfloat16 [2048, 1536], replicated, may hold values from -0.125 to 0.125
- view_order: int32 [8, 4], P('seq'), may hold values from 0 to 3, each once within a row
- tile_order: int32 [8, 4], P('seq'), may hold values from 0 to 3, each once within a row
Outputs:
- next_tokens: bfloat16 [8, 4, 512, 1536], P('seq', 'view')
The draws below stay inside these ranges and needn't reach their ends.
Inputs may be any that keep to these rules, and one draw needn't show every extreme that they name: `log_decay`: negative everywhere. `view_order`: each row is a permutation of the views. `tile_order`: each row is a permutation of the tiles of a block.
All inputs are finite; a program needn't handle non-finite values.
Results may differ from the reference program's by a relative error of at most 0.0059.
Values may be sent and summed in bfloat16 or wider, within the bound.
A program may use at most 128 MiB of HBM per device.

```python
import jax
import jax.numpy as jnp
from jax import lax

H = 32
HEAD = 64
N = 128
D_OUT = 1536
GROUP = 256
TILE = 128
TOKENS_PER_BLOCK = 512
DI = 2048
BAND_TOTAL = 8
VIEW_TOTAL = 4
PIECE = 64
TILES_DEV = 4


def draw_ssd_input(key, part):
    random_subkeys = jax.random.split(key, 3)
    channel_scale = jnp.exp(jax.random.uniform(random_subkeys[0], (H * HEAD,), jnp.float32, jnp.log(0.3), jnp.log(3.0)))
    token_scale = jnp.exp(jax.random.uniform(random_subkeys[1], (BAND_TOTAL, VIEW_TOTAL, TOKENS_PER_BLOCK, 1), jnp.float32, jnp.log(0.6), jnp.log(1.7)))
    values = jnp.clip(jax.random.normal(random_subkeys[2], (BAND_TOTAL, VIEW_TOTAL, TOKENS_PER_BLOCK, H * HEAD), jnp.float32), -4.0, 4.0)
    return (values * token_scale * channel_scale).astype(jnp.bfloat16)


def draw_log_decay(key, part):
    random_subkeys = jax.random.split(key, 7)
    sequence_length = BAND_TOTAL * VIEW_TOTAL * TOKENS_PER_BLOCK
    fast_share = 0.5
    fast_heads = jax.random.uniform(random_subkeys[0], (H,), jnp.float32) < fast_share
    slow_rate = jnp.exp(jax.random.uniform(random_subkeys[1], (H,), jnp.float32, jnp.log(0.1), jnp.log(0.5))) / sequence_length
    fast_rate = jnp.exp(jax.random.uniform(random_subkeys[2], (H,), jnp.float32, jnp.log(1.0 / 60.0), jnp.log(1.0 / 25.0)))
    head_decay_rate = jnp.where(fast_heads, fast_rate, slow_rate)
    block_multiplier = jnp.exp(jax.random.uniform(random_subkeys[3], (BAND_TOTAL, VIEW_TOTAL, 1, 1), jnp.float32, jnp.log(0.5), jnp.log(2.0)))
    token_multiplier = jnp.exp(jax.random.uniform(random_subkeys[4], (BAND_TOTAL, VIEW_TOTAL, H, TOKENS_PER_BLOCK), jnp.float32, jnp.log(0.5), jnp.log(2.0)))
    spike_positions = jax.random.randint(random_subkeys[5], (3,), 0, sequence_length)
    spike_keep_mask = jnp.log(jax.random.uniform(random_subkeys[6], (3,), jnp.float32, 0.6, 0.8))
    token_positions = jnp.arange(sequence_length, dtype=jnp.int32).reshape(BAND_TOTAL, VIEW_TOTAL, 1, TOKENS_PER_BLOCK)
    spike_log_decay = jnp.zeros((BAND_TOTAL, VIEW_TOTAL, 1, TOKENS_PER_BLOCK), jnp.float32)
    for lookup_index in range(3):
        spike_log_decay = spike_log_decay + jnp.where(token_positions == spike_positions[lookup_index], spike_keep_mask[lookup_index], 0.0)
    return -head_decay_rate[None, None, :, None] * block_multiplier * token_multiplier + spike_log_decay


def block_scale(rng, shape, shards, smallest, top_value):
    def one(axis_at, shards_of):
        steps = jax.random.uniform(jax.random.fold_in(jax.random.fold_in(rng, 6), axis_at), (shards_of,), jnp.float32, smallest / len(shards), top_value / len(shards))
        return jnp.repeat(jnp.exp(steps), shape[axis_at] // shards_of).reshape((-1,) + (1,) * (len(shape) - axis_at - 1))

    gain = one(*shards[0])
    for cut in shards[1:]:
        gain = gain * one(*cut)
    return gain


def normal_values(stream_key, dims, deviation, bound, shards=(), held_as=jnp.bfloat16):
    drawn = deviation * jax.random.normal(stream_key, dims, jnp.float32)
    if shards:
        drawn = drawn * block_scale(stream_key, dims, shards, -0.22, 0.18)
    return jnp.clip(drawn, -bound, bound).astype(held_as)


def setup_inputs(seed: int = 0) -> dict:
    key_list = jax.random.split(jax.random.key(seed), 11)
    return {
        "ssd_input": draw_ssd_input(jax.random.fold_in(key_list[10], 71), 0),
        "gate_input": normal_values(key_list[1], (BAND_TOTAL, VIEW_TOTAL, TOKENS_PER_BLOCK, DI), 1.0, 6.0, ((0, 8), (1, 4))),
        "b_matrix": normal_values(key_list[2], (BAND_TOTAL, VIEW_TOTAL, TOKENS_PER_BLOCK, N), 1.0, 6.0, ((0, 8), (1, 4))),
        "c_matrix": normal_values(key_list[3], (BAND_TOTAL, VIEW_TOTAL, TOKENS_PER_BLOCK, N), 0.088, 0.52734375, ((0, 8), (1, 4))),
        "log_decay": draw_log_decay(jax.random.fold_in(key_list[10], 71), 0),
        "d_skip": jnp.clip(jax.random.uniform(key_list[5], (H,), jnp.float32, 1.0, 4.0), 1.0, 4.0),
        "norm_gain": jnp.clip(1.0 + 0.18 * jax.random.normal(key_list[6], (DI,), jnp.float32), 0.1, 1.9),
        "out_weight": normal_values(key_list[7], (DI, D_OUT), DI ** -0.5, 0.125),
        "view_order": jax.vmap(lambda own: jax.random.permutation(own, VIEW_TOTAL))(jax.random.split(key_list[8], BAND_TOTAL)).reshape((BAND_TOTAL, VIEW_TOTAL)).astype(jnp.int32),
        "tile_order": jax.vmap(lambda own: jax.random.permutation(own, TILES_DEV))(jax.random.split(key_list[9], BAND_TOTAL)).reshape((BAND_TOTAL, TILES_DEV)).astype(jnp.int32),
    }


EPS = 1e-05

def group_parts(x_block, b_block, c_block, g_block):
    group_count = TOKENS_PER_BLOCK // GROUP
    cum_log = jnp.cumsum(g_block.reshape(H, group_count, GROUP), axis=2)
    group_end = cum_log[:, :, GROUP - 1]
    x_groups = x_block.reshape(group_count, GROUP, H, HEAD).astype(jnp.float32)
    b_groups = b_block.reshape(group_count, GROUP, N).astype(jnp.float32)
    c_groups = c_block.reshape(group_count, GROUP, N).astype(jnp.float32)
    return (cum_log, group_end, x_groups, b_groups, c_groups)

def group_states(cum_log, group_end, x_groups, b_groups):
    scaled = jnp.exp(group_end[:, :, None] - cum_log)[..., None] * b_groups[None]
    scaled = lax.optimization_barrier(scaled.astype(jnp.bfloat16)).astype(jnp.float32)
    return jnp.einsum('hckn,ckhp->hcpn', scaled, x_groups)

def summary(block):
    x_block, b_block, c_block, g_block = block
    cum_log, group_end, x_groups, b_groups, c_groups = group_parts(x_block, b_block, c_block, g_block)
    states = group_states(cum_log, group_end, x_groups, b_groups)
    group_decay = jnp.exp(group_end)
    total = jnp.ones((H,), jnp.float32)
    running = jnp.zeros((H, HEAD, N), jnp.float32)
    for lookup_index in range(TOKENS_PER_BLOCK // GROUP):
        running = group_decay[:, lookup_index, None, None] * running + states[:, lookup_index]
        total = total * group_decay[:, lookup_index]
    return (total, running)

def reference(ssd_input, gate_input, b_matrix, c_matrix, log_decay, d_skip, norm_gain, out_weight, view_order, tile_order):
    group_count = TOKENS_PER_BLOCK // GROUP
    blocks = BAND_TOTAL * VIEW_TOTAL
    x_all = ssd_input.reshape(blocks, TOKENS_PER_BLOCK, H * HEAD)
    z_all = gate_input.reshape(blocks, TOKENS_PER_BLOCK, H * HEAD)
    b_all = b_matrix.reshape(blocks, TOKENS_PER_BLOCK, N)
    c_all = c_matrix.reshape(blocks, TOKENS_PER_BLOCK, N)
    g_all = log_decay.reshape(blocks, H, TOKENS_PER_BLOCK)
    totals, states = lax.map(summary, (x_all, b_all, c_all, g_all))
    totals = totals.reshape(BAND_TOTAL, VIEW_TOTAL, H)
    states = states.reshape(BAND_TOTAL, VIEW_TOTAL, H, HEAD, N)

    def row_step(carry, row):
        row_totals, row_states, row_order = row
        entering = jnp.zeros((VIEW_TOTAL, H, HEAD, N), jnp.float32)
        for rank_pos in range(VIEW_TOTAL):
            view_now = row_order[rank_pos]
            entering = entering.at[view_now].set(carry)
            carry = jnp.take(row_totals, view_now, axis=0)[:, None, None] * carry + jnp.take(row_states, view_now, axis=0)
        return (carry, entering)
    _, entering = lax.scan(row_step, jnp.zeros((H, HEAD, N), jnp.float32), (totals, states, view_order))
    entering = entering.reshape(blocks, H, HEAD, N)
    causal = jnp.tril(jnp.ones((GROUP, GROUP), dtype=bool))

    def block_out(block):
        x_block, z_block, b_block, c_block, g_block, start = block
        cum_log, group_end, x_groups, b_groups, c_groups = group_parts(x_block, b_block, c_block, g_block)
        states_here = group_states(cum_log, group_end, x_groups, b_groups)
        group_decay = jnp.exp(group_end)
        scores = jnp.einsum('cqn,ckn->cqk', c_groups, b_groups)
        log_gaps = cum_log[:, :, :, None] - cum_log[:, :, None, :]
        weights = jnp.exp(jnp.where(causal, log_gaps, -jnp.inf)) * scores[None]
        weights = lax.optimization_barrier(weights.astype(jnp.bfloat16)).astype(jnp.float32)
        inside = jnp.einsum('hcqk,ckhp->cqhp', weights, x_groups)
        running = start
        collected = []
        for lookup_index in range(group_count):
            collected.append(running)
            running = group_decay[:, lookup_index, None, None] * running + states_here[:, lookup_index]
        entry = jnp.stack(collected, axis=1)
        entry = lax.optimization_barrier(entry.astype(jnp.bfloat16)).astype(jnp.float32)
        carried = jnp.einsum('cqn,hcpn->cqhp', c_groups, entry) * jnp.transpose(jnp.exp(cum_log), (1, 2, 0))[..., None]
        mixed = inside + carried + d_skip[None, None, :, None] * x_groups
        gate_vals = z_block.reshape(group_count, GROUP, H, HEAD).astype(jnp.float32)
        gated = mixed * jax.nn.silu(gate_vals)
        inv_rms = lax.rsqrt(lax.optimization_barrier(jnp.mean(gated * gated, axis=-1, keepdims=True)) + EPS)
        normed = (gated * inv_rms * norm_gain.reshape(H, HEAD)).astype(jnp.bfloat16).reshape(TOKENS_PER_BLOCK, H * HEAD)
        return jnp.dot(normed, out_weight, preferred_element_type=jnp.float32).astype(jnp.bfloat16)
    projected = lax.map(block_out, (x_all, z_all, b_all, c_all, g_all, entering))
    projected = projected.reshape(BAND_TOTAL, VIEW_TOTAL, BAND_TOTAL, PIECE, D_OUT)
    reordered = jnp.transpose(projected, (2, 1, 0, 3, 4)).reshape(BAND_TOTAL, VIEW_TOTAL, TILES_DEV, TILE, D_OUT)
    picked = jax.vmap(lambda band_rows, order_row: jnp.take(band_rows, order_row, axis=1))(reordered, tile_order)
    return picked.reshape(BAND_TOTAL, VIEW_TOTAL, TOKENS_PER_BLOCK, D_OUT)
```

```python
import functools

import jax
import jax.numpy as jnp
from jax import lax
from jax.experimental import pallas as pl
from jax.experimental.pallas import tpu as pltpu
from jax.sharding import PartitionSpec as P

GROUP = 256
TILE = 128
EPS = 1e-05
MESH = pl.DeviceIdType.MESH
F32 = jnp.float32
BF16 = jnp.bfloat16
VMEM = pltpu.VMEM


def nn(a, b):
    return lax.dot_general(a, b, (((1,), (0,)), ((), ())), preferred_element_type=F32)


def nt(a, b):
    return lax.dot_general(a, b, (((1,), (1,)), ((), ())), preferred_element_type=F32)


def tn(a, b):
    return lax.dot_general(a, b, (((0,), (0,)), ((), ())), preferred_element_type=F32)


def split3(a):
    hi = a.astype(BF16)
    rest = a - hi.astype(F32)
    mid = rest.astype(BF16)
    low = (rest - mid.astype(F32)).astype(BF16)
    return hi, mid, low


def iota(shape, dim):
    return lax.broadcasted_iota(jnp.int32, shape, dim)


def pair_columns(full, pair):
    lanes = full.shape[1]
    turned = pltpu.roll(full, lax.rem(lanes - 2 * pair, lanes), 1)
    return turned[:, 0:1], turned[:, 1:2]


def local_kernel(
    x_ref, b_ref, c_ref, ld_ref, skip_ref,
    inside_ref, state_ref, prefix_ref, ecol_ref, total_ref,
    row_s, col_s, score_s,
):
    pair = pl.program_id(0)
    heads, tokens = ld_ref.shape
    groups = tokens // GROUP

    @pl.when(pair == 0)
    def _():
        at_row, at_col = iota((GROUP, GROUP), 0), iota((GROUP, GROUP), 1)
        lower = jnp.where(at_col <= at_row, 1.0, 0.0).astype(BF16)
        upper = jnp.where(at_row <= at_col, 1.0, 0.0).astype(BF16)
        total = jnp.zeros((heads, 1), F32)
        for c in range(groups):
            span = slice(c * GROUP, (c + 1) * GROUP)
            own = ld_ref[:, span]
            padded = jnp.concatenate([own, jnp.zeros((128 - heads, GROUP), F32)], axis=0)
            rows = sum(nn(part, upper) for part in split3(own))
            row_s[:, span] = rows
            cols = sum(nt(lower, part) for part in split3(padded))
            col_s[span, :] = cols
            ecol_ref[span, :] = jnp.exp(cols)
            total = total + rows[:, GROUP - 1 : GROUP]
            scores = nt(c_ref[span, :], b_ref[span, :])
            score_s[c] = jnp.where(at_col <= at_row, scores, 0.0)
        total_ref[...] = jnp.broadcast_to(total, total_ref.shape)

    first_half = iota((GROUP, 128), 1) < 64
    top_half = iota((128, 128), 0) < 64
    col0, col1 = pair_columns(col_s[...], pair)
    running = jnp.zeros((128, 128), F32)
    for c in range(groups):
        span = slice(c * GROUP, (c + 1) * GROUP)
        x = x_ref[span, :]
        xf = x.astype(F32)
        outs = []
        ends = []
        for j, col in enumerate((col0, col1)):
            row = row_s[pl.ds(2 * pair + j, 1), span]
            mine = col[span, :]
            gap = jnp.minimum(mine - row, 0.0)
            weights = (jnp.exp(gap) * score_s[c]).astype(BF16)
            outs.append(nn(weights, x))
            ends.append(mine[GROUP - 1 : GROUP, :])
        inside_ref[span, :] = jnp.where(first_half, outs[0], outs[1]) + skip_ref[...] * xf
        factor = jnp.where(first_half, ends[0] - col0[span, :], ends[1] - col1[span, :])
        scaled = (xf * jnp.exp(jnp.minimum(factor, 0.0))).astype(BF16)
        state = tn(scaled, b_ref[span, :])
        if c:
            prefix_ref[c - 1] = running
        decay = jnp.exp(jnp.where(top_half, ends[0], ends[1]))
        running = decay * running + state
    state_ref[...] = running.astype(BF16)


def local_part(x, b, c, ld, skip):
    tokens, width = x.shape
    heads = ld.shape[0]
    groups = tokens // GROUP
    pairs = width // 128
    whole = lambda shape: pl.BlockSpec(shape, lambda p: (0,) * len(shape))
    lanes = lambda rows: pl.BlockSpec((rows, 128), lambda p: (0, p))
    return pl.pallas_call(
        local_kernel,
        grid=(pairs,),
        in_specs=[lanes(tokens), whole(b.shape), whole(c.shape), whole(ld.shape), lanes(1)],
        out_specs=[
            lanes(tokens),
            pl.BlockSpec((128, 128), lambda p: (p, 0)),
            pl.BlockSpec((groups - 1, 128, 128), lambda p: (0, p, 0)),
            whole((tokens, 128)),
            whole((heads, 128)),
        ],
        out_shape=[
            jax.ShapeDtypeStruct((tokens, width), F32),
            jax.ShapeDtypeStruct((width, 128), BF16),
            jax.ShapeDtypeStruct((groups - 1, width, 128), F32),
            jax.ShapeDtypeStruct((tokens, 128), F32),
            jax.ShapeDtypeStruct((heads, 128), F32),
        ],
        scratch_shapes=[
            VMEM((heads, tokens), F32),
            VMEM((tokens, 128), F32),
            VMEM((groups, GROUP, GROUP), F32),
        ],
        name="local_part",
    )(x, b, c, ld, skip)


def scan_kernel(
    views, pack, groups, share,
    order_ref, state_ref, total_ref, out_ref,
    note_s, got_s, gotnote_s, agg_s, aggnote_s, aggs_s, aggnotes_s, within_s, before_s, send_s,
    sem_a, sem_an, sem_b, sem_bn, sem_c,
):
    band, view = lax.axis_index("seq"), lax.axis_index("view")
    count = views * pack
    group, member = band // pack, lax.rem(band, pack)
    me = member * views + view
    rows = share * 64

    def peer(q):
        return {"seq": group * pack + q // views, "view": lax.rem(q, views)}

    def across(g):
        return {"seq": g * pack + member, "view": view}

    barrier = pltpu.get_barrier_semaphore()
    for d in range(1, count):
        pl.semaphore_signal(
            barrier, inc=1, device_id=peer(lax.rem(me + d, count)), device_id_type=MESH
        )
    for d in range(1, groups):
        pl.semaphore_signal(
            barrier, inc=1, device_id=across(lax.rem(group + d, groups)), device_id_type=MESH
        )
    rank = jnp.int32(0)
    for r in range(views):
        rank = rank + jnp.where(order_ref[0, r] == view, r, 0)
    key = (rank + member * views).astype(F32)
    for q in range(count):
        note_s[q, 0:share, :] = total_ref[q * share : (q + 1) * share, :]
        note_s[q, share : share + 1, :] = jnp.full((1, 128), key, F32)
    pl.semaphore_wait(barrier, count - 1 + groups - 1)

    def exchange(source, target, sem, d, q):
        return pltpu.make_async_remote_copy(
            src_ref=source, dst_ref=target, send_sem=sem.at[0, d], recv_sem=sem.at[1, d],
            device_id=peer(q), device_id_type=MESH,
        )

    sends = []
    for d in range(1, count):
        q = lax.rem(me + d, count)
        sends.append(exchange(note_s.at[q], gotnote_s.at[me], sem_an, d, q))
        sends[-1].start()
        sends.append(exchange(state_ref.at[q], got_s.at[me], sem_a, d, q))
        sends[-1].start()
    got_s[me] = state_ref[me]
    gotnote_s[me] = note_s[me]
    for d in range(1, count):
        src = lax.rem(me - d + count, count)
        exchange(note_s.at[src], gotnote_s.at[src], sem_an, d, src).wait_recv()
        exchange(state_ref.at[src], got_s.at[src], sem_a, d, src).wait_recv()

    logs = [gotnote_s[b] for b in range(count)]
    keys = [jnp.broadcast_to(log[share : share + 1, :], log.shape) for log in logs]
    zero = jnp.zeros_like(logs[0])
    before, upto, whole = [], [], zero
    for b in range(count):
        acc = zero
        for o in range(count):
            if o != b:
                acc = acc + jnp.where(keys[o] < keys[b], logs[o], 0.0)
        before.append(acc)
        upto.append(acc + logs[b])
        before_s[b] = jnp.exp(acc)
        whole = whole + logs[b]
    aggnote_s[...] = whole
    last = [jnp.exp(jnp.minimum(whole - upto[b], 0.0)) for b in range(count)]
    for i in range(share):
        span = slice(i * 64, (i + 1) * 64)
        acc = jnp.zeros((64, 128), F32)
        for b in range(count):
            acc = acc + last[b][i : i + 1, :] * got_s[b, span, :].astype(F32)
        agg_s[span, :] = acc.astype(BF16)

    def ahead(source, target, sem, k, g):
        return pltpu.make_async_remote_copy(
            src_ref=source, dst_ref=target, send_sem=sem.at[0, k], recv_sem=sem.at[1, k],
            device_id=across(g), device_id_type=MESH,
        )

    def ahead_pair(k, g):
        return (
            ahead(aggnote_s, aggnotes_s.at[k], sem_bn, k, g),
            ahead(agg_s, aggs_s.at[k], sem_b, k, g),
        )

    for k in range(groups - 1, 0, -1):
        @pl.when(group + k < groups)
        def _(k=k):
            for copy in ahead_pair(k, group + k):
                copy.start()

    for b in range(count):
        coefs = [
            jnp.where(
                keys[o] < keys[b], jnp.exp(jnp.minimum(before[b] - upto[o], 0.0)), 0.0
            )
            for o in range(count)
            if o != b
        ]
        others = [o for o in range(count) if o != b]
        for i in range(share):
            span = slice(i * 64, (i + 1) * 64)
            acc = jnp.zeros((64, 128), F32)
            for o, coef in zip(others, coefs):
                acc = acc + coef[i : i + 1, :] * got_s[o, span, :].astype(F32)
            within_s[b, span, :] = acc

    carry = within_s.at[count]
    carry[...] = jnp.zeros((rows, 128), F32)
    for k in range(groups - 1, 0, -1):
        @pl.when(group - k >= 0)
        def _(k=k):
            for copy in ahead_pair(k, group - k):
                copy.wait_recv()
            decay = jnp.exp(aggnotes_s[k])
            for i in range(share):
                span = slice(i * 64, (i + 1) * 64)
                carry[span, :] = decay[i : i + 1, :] * carry[span, :] + aggs_s[k, span, :].astype(F32)

    def entering(q):
        factor = before_s[q]
        parts = []
        for i in range(share):
            span = slice(i * 64, (i + 1) * 64)
            parts.append(factor[i : i + 1, :] * carry[span, :] + within_s[q, span, :])
        return jnp.concatenate(parts, axis=0).astype(BF16)

    for d in range(1, count):
        q = lax.rem(me + d, count)
        send_s[d] = entering(q)
        sends.append(exchange(send_s.at[d], out_ref.at[me], sem_c, d, q))
        sends[-1].start()
    out_ref[me] = entering(me)
    for d in range(1, count):
        src = lax.rem(me - d + count, count)
        exchange(send_s.at[d], out_ref.at[src], sem_c, d, src).wait_recv()
    for copy in sends:
        copy.wait_send()
    for k in range(1, groups):
        @pl.when(group + k < groups)
        def _(k=k):
            for copy in ahead_pair(k, group + k):
                copy.wait_send()


def scan_part(order, state, total, views, bands):
    heads = total.shape[0]
    pack = 2 if bands % 2 == 0 and heads % (2 * views) == 0 else 1
    count = views * pack
    share = heads // count
    groups = bands // pack
    rows = share * 64
    vmem = pl.BlockSpec(memory_space=pltpu.VMEM)
    sems = lambda n: pltpu.SemaphoreType.DMA((2, n))
    return pl.pallas_call(
        functools.partial(scan_kernel, views, pack, groups, share),
        in_specs=[pl.BlockSpec(memory_space=pltpu.SMEM), vmem, vmem],
        out_specs=vmem,
        out_shape=jax.ShapeDtypeStruct((count, rows, 128), BF16),
        scratch_shapes=[
            VMEM((count, 8, 128), F32),
            VMEM((count, rows, 128), BF16),
            VMEM((count, 8, 128), F32),
            VMEM((rows, 128), BF16),
            VMEM((8, 128), F32),
            VMEM((groups, rows, 128), BF16),
            VMEM((groups, 8, 128), F32),
            VMEM((count + 1, rows, 128), F32),
            VMEM((count, 8, 128), F32),
            VMEM((count, rows, 128), BF16),
            sems(count), sems(count), sems(groups), sems(groups), sems(count),
        ],
        compiler_params=pltpu.CompilerParams(collective_id=0, has_side_effects=True),
        name="scan_part",
    )(order, state.reshape(count, rows, 128), total)


def token_kernel(
    inside_ref, gate_ref, ent_ref, prefix_ref, ecol_ref, c_ref, gain_ref, w_hbm, out_ref,
    normed_s, w_s, sem,
):
    pair = pl.program_id(0)
    tokens = inside_ref.shape[0]
    groups = tokens // GROUP
    width_out = out_ref.shape[1]
    load = pltpu.make_async_copy(w_hbm, w_s, sem)

    @pl.when(pair == 0)
    def _():
        load.start()

    first_half = iota((GROUP, 128), 1) < 64
    top_half = iota((128, 128), 0) < 64
    same = (iota((128, 128), 0) < 64) == (iota((128, 128), 1) < 64)
    block = jnp.where(same, 1.0 / 64.0, 0.0).astype(BF16)
    e0, e1 = pair_columns(ecol_ref[...], pair)
    base = ent_ref[...].astype(F32)
    before = jnp.ones((128, 128), F32)
    for c in range(groups):
        span = slice(c * GROUP, (c + 1) * GROUP)
        entry = (before * base + prefix_ref[c - 1]).astype(BF16) if c else ent_ref[...]
        end = (c + 1) * GROUP
        before = before * jnp.where(top_half, e0[end - 1 : end, :], e1[end - 1 : end, :])
        carried = nt(c_ref[span, :], entry)
        carried = carried * jnp.where(first_half, e0[span, :], e1[span, :])
        gate = gate_ref[span, :].astype(F32)
        g = (inside_ref[span, :] + carried) * (gate / (1.0 + jnp.exp(-gate)))
        square = g * g
        high = square.astype(BF16)
        low = (square - high.astype(F32)).astype(BF16)
        mean = nn(high, block) + nn(low, block)
        normed = g * lax.rsqrt(mean + EPS) * gain_ref[...]
        normed_s[span, pl.ds(pl.multiple_of(pair * 128, 128), 128)] = normed.astype(BF16)

    @pl.when(pair == pl.num_programs(0) - 1)
    def _():
        load.wait()

        @pl.loop(0, width_out // 256)
        def _(n):
            cols = pl.ds(pl.multiple_of(n * 256, 256), 256)
            out_ref[:, cols] = nn(normed_s[...], w_s[:, cols]).astype(BF16)


def token_part(inside, gate, ent, prefix, ecol, c, gain, w):
    tokens, width = inside.shape
    pairs = width // 128
    whole = lambda shape: pl.BlockSpec(shape, lambda p: (0,) * len(shape))
    lanes = lambda rows: pl.BlockSpec((rows, 128), lambda p: (0, p))
    return pl.pallas_call(
        token_kernel,
        grid=(pairs,),
        in_specs=[
            lanes(tokens),
            lanes(tokens),
            pl.BlockSpec((128, 128), lambda p: (p, 0)),
            pl.BlockSpec((prefix.shape[0], 128, 128), lambda p: (0, p, 0)),
            whole(ecol.shape),
            whole(c.shape),
            lanes(1),
            pl.BlockSpec(memory_space=pl.ANY),
        ],
        out_specs=whole((tokens, w.shape[1])),
        out_shape=jax.ShapeDtypeStruct((tokens, w.shape[1]), BF16),
        scratch_shapes=[
            VMEM((tokens, width), BF16),
            VMEM(w.shape, BF16),
            pltpu.SemaphoreType.DMA,
        ],
        compiler_params=pltpu.CompilerParams(vmem_limit_bytes=40 * 1024 * 1024),
        name="token_part",
    )(inside, gate, ent, prefix, ecol, c, gain, w)


def swap_kernel(bands, tile_ref, mine_ref, out_ref, got_s, sem):
    band, view = lax.axis_index("seq"), lax.axis_index("view")
    barrier = pltpu.get_barrier_semaphore()

    def to(j):
        return {"seq": j, "view": view}

    for d in range(1, bands):
        pl.semaphore_signal(
            barrier, inc=1, device_id=to(lax.rem(band + d, bands)), device_id_type=MESH
        )
    pl.semaphore_wait(barrier, bands - 1)

    def copy(source, target, d, j):
        return pltpu.make_async_remote_copy(
            src_ref=source, dst_ref=target, send_sem=sem.at[0, d], recv_sem=sem.at[1, d],
            device_id=to(j), device_id_type=MESH,
        )

    sends = []
    for d in sorted(range(1, bands), key=lambda d: -min(d, bands - d)):
        j = lax.rem(band + d, bands)
        sends.append(copy(mine_ref.at[j], got_s.at[band], d, j))
        sends[-1].start()
    got_s[band] = mine_ref[band]
    for d in range(1, bands):
        i = lax.rem(band - d + bands, bands)
        copy(mine_ref.at[i], got_s.at[i], d, i).wait_recv()
    for k in range(out_ref.shape[0]):
        per = out_ref.shape[1]
        tile = tile_ref[0, k]
        for u in range(per):
            out_ref[k, u] = got_s[tile * per + u]
    for sent in sends:
        sent.wait_send()


def swap_part(tiles, projected, bands):
    tokens, width = projected.shape
    piece = tokens // bands
    per = TILE // piece
    vmem = pl.BlockSpec(memory_space=pltpu.VMEM)
    return pl.pallas_call(
        functools.partial(swap_kernel, bands),
        in_specs=[pl.BlockSpec(memory_space=pltpu.SMEM), vmem],
        out_specs=vmem,
        out_shape=jax.ShapeDtypeStruct((tokens // TILE, per, piece, width), BF16),
        scratch_shapes=[
            VMEM((bands, piece, width), BF16),
            pltpu.SemaphoreType.DMA((2, bands)),
        ],
        compiler_params=pltpu.CompilerParams(collective_id=1, has_side_effects=True),
        name="swap_part",
    )(tiles, projected.reshape(bands, piece, width))


def shards(
    ssd_input, gate_input, b_matrix, c_matrix, log_decay,
    d_skip, norm_gain, out_weight, view_order, tile_order,
):
    views, bands = lax.axis_size("view"), lax.axis_size("seq")
    x, gate = ssd_input[0, 0], gate_input[0, 0]
    b, c, ld = b_matrix[0, 0], c_matrix[0, 0], log_decay[0, 0]
    tokens, width = x.shape
    skip = jnp.repeat(d_skip, width // d_skip.shape[0])[None, :]
    inside, state, prefix, ecol, total = local_part(x, b, c, ld, skip)
    ent = scan_part(view_order, state, total, views, bands).reshape(width, 128)
    projected = token_part(inside, gate, ent, prefix, ecol, c, norm_gain[None, :], out_weight)
    out = swap_part(tile_order, projected, bands)
    return out.reshape(1, 1, tokens, out_weight.shape[1])


def solution(mesh):
    whole = P("seq", "view", None, None)
    in_specs = (whole,) * 5 + (P(), P(), P(), P("seq", None), P("seq", None))
    return jax.shard_map(
        shards, mesh=mesh, in_specs=in_specs, out_specs=whole, check_vma=False
    )
```

```python
import functools

import jax
import jax.numpy as jnp
from jax import lax
from jax.experimental import pallas as pl
from jax.experimental.pallas import tpu as pltpu
from jax.sharding import PartitionSpec as P

GROUP = 256
TILE = 128
EPS = 1e-05
MESH = pl.DeviceIdType.MESH
F32 = jnp.float32
BF16 = jnp.bfloat16
VMEM = pltpu.VMEM
VMEM_LIMIT = 64 * 1000 * 1000


def nn(a, b):
    return lax.dot_general(a, b, (((1,), (0,)), ((), ())), preferred_element_type=F32)


def nt(a, b):
    return lax.dot_general(a, b, (((1,), (1,)), ((), ())), preferred_element_type=F32)


def tn(a, b):
    return lax.dot_general(a, b, (((0,), (0,)), ((), ())), preferred_element_type=F32)


def split3(a):
    hi = a.astype(BF16)
    rest = a - hi.astype(F32)
    mid = rest.astype(BF16)
    low = (rest - mid.astype(F32)).astype(BF16)
    return hi, mid, low


def iota(shape, dim):
    return lax.broadcasted_iota(jnp.int32, shape, dim)


def pair_columns(full, pair):
    lanes = full.shape[1]
    turned = pltpu.roll(full, lax.rem(lanes - 2 * pair, lanes), 1)
    return turned[:, 0:1], turned[:, 1:2]


def local_kernel(
    x_ref, b_ref, c_ref, ld_ref,
    state_ref, prefix_ref, col_ref, row_ref, score_ref, total_ref,
    scale_s,
):
    step = pl.program_id(0)
    heads, tokens = ld_ref.shape
    groups = tokens // GROUP
    pairs = x_ref.shape[1] // 128

    @pl.when(step == 0)
    def _():
        at_row, at_col = iota((GROUP, GROUP), 0), iota((GROUP, GROUP), 1)
        lower = jnp.where(at_col <= at_row, 1.0, 0.0).astype(BF16)
        upper = jnp.where(at_row <= at_col, 1.0, 0.0).astype(BF16)
        total = jnp.zeros((heads, 1), F32)
        for c in range(groups):
            span = slice(c * GROUP, (c + 1) * GROUP)
            own = ld_ref[:, span]
            padded = jnp.concatenate([own, jnp.zeros((128 - heads, GROUP), F32)], axis=0)
            rows = sum(nn(part, upper) for part in split3(own))
            row_ref[:, span] = rows
            cols = sum(nt(lower, part) for part in split3(padded))
            col_ref[span, :] = cols
            scale_s[span, :] = jnp.exp(jnp.minimum(cols[GROUP - 1 : GROUP, :] - cols, 0.0))
            total = total + rows[:, GROUP - 1 : GROUP]
            scores = nt(c_ref[span, :], b_ref[span, :])
            score_ref[c] = jnp.where(at_col <= at_row, scores, 0.0)
        total_ref[...] = jnp.broadcast_to(total, total_ref.shape)

    top_half = iota((128, 128), 0) < 64
    for j in range(pairs):
        pair = step * pairs + j
        at = slice(j * 128, (j + 1) * 128)
        f0, f1 = pair_columns(scale_s[...], pair)
        running = jnp.zeros((128, 128), F32)
        for c in range(groups):
            span = slice(c * GROUP, (c + 1) * GROUP)
            bf = b_ref[span, :].astype(F32)
            scaled = jnp.concatenate(
                [(f0[span, :] * bf).astype(BF16), (f1[span, :] * bf).astype(BF16)], axis=1
            )
            both = tn(x_ref[span, at], scaled)
            state = jnp.where(top_half, both[:, 0:128], both[:, 128:256])
            if c:
                prefix_ref[c - 1, at, :] = running
            e0 = row_ref[pl.ds(2 * pair, 1), span][:, GROUP - 1 : GROUP]
            e1 = row_ref[pl.ds(2 * pair + 1, 1), span][:, GROUP - 1 : GROUP]
            running = jnp.exp(jnp.where(top_half, e0, e1)) * running + state
        state_ref[at, :] = running.astype(BF16)


def local_part(x, b, c, ld):
    tokens, width = x.shape
    heads = ld.shape[0]
    groups = tokens // GROUP
    block = 512
    whole = lambda shape: pl.BlockSpec(shape, lambda p: (0,) * len(shape))
    shapes = [
        ((width, 128), BF16, pl.BlockSpec((block, 128), lambda p: (p, 0))),
        ((groups - 1, width, 128), F32, pl.BlockSpec((groups - 1, block, 128), lambda p: (0, p, 0))),
        ((tokens, 128), F32, whole((tokens, 128))),
        ((heads, tokens), F32, whole((heads, tokens))),
        ((groups, GROUP, GROUP), F32, whole((groups, GROUP, GROUP))),
        ((heads, 128), F32, whole((heads, 128))),
    ]
    return pl.pallas_call(
        local_kernel,
        grid=(width // block,),
        in_specs=[
            pl.BlockSpec((tokens, block), lambda p: (0, p)),
            whole(b.shape), whole(c.shape), whole(ld.shape),
        ],
        out_specs=[spec for _, _, spec in shapes],
        out_shape=[jax.ShapeDtypeStruct(shape, dtype) for shape, dtype, _ in shapes],
        scratch_shapes=[VMEM((tokens, 128), F32)],
        compiler_params=pltpu.CompilerParams(vmem_limit_bytes=VMEM_LIMIT),
        name="local_part",
    )(x, b, c, ld)


def scan_kernel(
    views, pack, groups, share,
    order_ref, state_ref, total_ref, skip_ref, col_ref, row_ref, score_ref, x_hbm,
    out_ref, inside_hbm,
    x_s, inside_s, sem_x, sem_i, note_s, got_s, gotnote_s, agg_s, aggnote_s, aggs_s, aggnotes_s, within_s, before_s, send_s,
    sem_a, sem_an, sem_b, sem_bn, sem_c,
):
    band, view = lax.axis_index("seq"), lax.axis_index("view")
    count = views * pack
    group, member = band // pack, lax.rem(band, pack)
    me = member * views + view
    rows = share * 64

    pairs = x_s.shape[1] // 128
    cuts = [0, pairs * 3 // 8, pairs * 11 // 16, pairs]
    load = pltpu.make_async_copy(x_hbm, x_s, sem_x)
    load.start()
    first_half = iota((GROUP, 128), 1) < 64

    def inside_span(part):
        @pl.loop(cuts[part], cuts[part + 1])
        def _(pair):
            cols = pair_columns(col_ref[...], pair)
            lanes = pl.ds(pl.multiple_of(pair * 128, 128), 128)
            for c in range(x_s.shape[0] // GROUP):
                span = slice(c * GROUP, (c + 1) * GROUP)
                x = x_s[span, lanes]
                outs = []
                for j, col in enumerate(cols):
                    line = row_ref[pl.ds(2 * pair + j, 1), span]
                    gap = jnp.minimum(col[span, :] - line, 0.0)
                    outs.append(nn((jnp.exp(gap) * score_ref[c]).astype(BF16), x))
                inside_s[span, lanes] = (
                    jnp.where(first_half, outs[0], outs[1])
                    + jnp.where(first_half, skip_ref[2 * pair], skip_ref[2 * pair + 1]) * x.astype(F32)
                )

        lanes = pl.ds(cuts[part] * 128, (cuts[part + 1] - cuts[part]) * 128)
        copy = pltpu.make_async_copy(
            inside_s.at[:, lanes], inside_hbm.at[:, lanes], sem_i.at[part]
        )
        copy.start()
        return copy

    def peer(q):
        return {"seq": group * pack + q // views, "view": lax.rem(q, views)}

    def across(g):
        return {"seq": g * pack + member, "view": view}

    barrier = pltpu.get_barrier_semaphore()
    for d in range(1, count):
        pl.semaphore_signal(
            barrier, inc=1, device_id=peer(lax.rem(me + d, count)), device_id_type=MESH
        )
    for d in range(1, groups):
        pl.semaphore_signal(
            barrier, inc=1, device_id=across(lax.rem(group + d, groups)), device_id_type=MESH
        )
    rank = jnp.int32(0)
    for r in range(views):
        rank = rank + jnp.where(order_ref[0, r] == view, r, 0)
    key = (rank + member * views).astype(F32)
    for q in range(count):
        note_s[q, 0:share, :] = total_ref[q * share : (q + 1) * share, :]
        note_s[q, share : share + 1, :] = jnp.full((1, 128), key, F32)
    pl.semaphore_wait(barrier, count - 1 + groups - 1)

    def exchange(source, target, sem, d, q):
        return pltpu.make_async_remote_copy(
            src_ref=source, dst_ref=target, send_sem=sem.at[0, d], recv_sem=sem.at[1, d],
            device_id=peer(q), device_id_type=MESH,
        )

    sends = []
    for d in range(1, count):
        q = lax.rem(me + d, count)
        sends.append(exchange(note_s.at[q], gotnote_s.at[me], sem_an, d, q))
        sends[-1].start()
        sends.append(exchange(state_ref.at[q], got_s.at[me], sem_a, d, q))
        sends[-1].start()
    got_s[me] = state_ref[me]
    gotnote_s[me] = note_s[me]
    load.wait()
    saved = [inside_span(0)]
    for d in range(1, count):
        src = lax.rem(me - d + count, count)
        exchange(note_s.at[src], gotnote_s.at[src], sem_an, d, src).wait_recv()
        exchange(state_ref.at[src], got_s.at[src], sem_a, d, src).wait_recv()

    logs = [gotnote_s[b] for b in range(count)]
    keys = [jnp.broadcast_to(log[share : share + 1, :], log.shape) for log in logs]
    zero = jnp.zeros_like(logs[0])
    before, upto, whole = [], [], zero
    for b in range(count):
        acc = zero
        for o in range(count):
            if o != b:
                acc = acc + jnp.where(keys[o] < keys[b], logs[o], 0.0)
        before.append(acc)
        upto.append(acc + logs[b])
        before_s[b] = jnp.exp(acc)
        whole = whole + logs[b]
    aggnote_s[...] = whole
    last = [jnp.exp(jnp.minimum(whole - upto[b], 0.0)) for b in range(count)]
    for i in range(share):
        span = slice(i * 64, (i + 1) * 64)
        acc = jnp.zeros((64, 128), F32)
        for b in range(count):
            acc = acc + last[b][i : i + 1, :] * got_s[b, span, :].astype(F32)
        agg_s[span, :] = acc.astype(BF16)

    def ahead(source, target, sem, k, g):
        return pltpu.make_async_remote_copy(
            src_ref=source, dst_ref=target, send_sem=sem.at[0, k], recv_sem=sem.at[1, k],
            device_id=across(g), device_id_type=MESH,
        )

    def ahead_pair(k, g):
        return (
            ahead(aggnote_s, aggnotes_s.at[k], sem_bn, k, g),
            ahead(agg_s, aggs_s.at[k], sem_b, k, g),
        )

    for k in range(groups - 1, 0, -1):
        @pl.when(group + k < groups)
        def _(k=k):
            for copy in ahead_pair(k, group + k):
                copy.start()

    for b in range(count):
        coefs = [
            jnp.where(
                keys[o] < keys[b], jnp.exp(jnp.minimum(before[b] - upto[o], 0.0)), 0.0
            )
            for o in range(count)
            if o != b
        ]
        others = [o for o in range(count) if o != b]
        for i in range(share):
            span = slice(i * 64, (i + 1) * 64)
            acc = jnp.zeros((64, 128), F32)
            for o, coef in zip(others, coefs):
                acc = acc + coef[i : i + 1, :] * got_s[o, span, :].astype(F32)
            within_s[b, span, :] = acc

    saved.append(inside_span(1))
    carry = within_s.at[count]
    carry[...] = jnp.zeros((rows, 128), F32)
    for k in range(groups - 1, 0, -1):
        @pl.when(group - k >= 0)
        def _(k=k):
            for copy in ahead_pair(k, group - k):
                copy.wait_recv()
            decay = jnp.exp(aggnotes_s[k])
            for i in range(share):
                span = slice(i * 64, (i + 1) * 64)
                carry[span, :] = decay[i : i + 1, :] * carry[span, :] + aggs_s[k, span, :].astype(F32)

    def entering(q):
        factor = before_s[q]
        parts = []
        for i in range(share):
            span = slice(i * 64, (i + 1) * 64)
            parts.append(factor[i : i + 1, :] * carry[span, :] + within_s[q, span, :])
        return jnp.concatenate(parts, axis=0).astype(BF16)

    for d in range(1, count):
        q = lax.rem(me + d, count)
        send_s[d] = entering(q)
        sends.append(exchange(send_s.at[d], out_ref.at[me], sem_c, d, q))
        sends[-1].start()
    out_ref[me] = entering(me)
    saved.append(inside_span(2))
    for d in range(1, count):
        src = lax.rem(me - d + count, count)
        exchange(send_s.at[d], out_ref.at[src], sem_c, d, src).wait_recv()
    for copy in sends:
        copy.wait_send()
    for k in range(1, groups):
        @pl.when(group + k < groups)
        def _(k=k):
            for copy in ahead_pair(k, group + k):
                copy.wait_send()
    for copy in saved:
        copy.wait()


def scan_part(order, state, total, col, row, score, skip, x, views, bands):
    heads = total.shape[0]
    pack = 2 if bands % 2 == 0 and heads % (2 * views) == 0 else 1
    count = views * pack
    share = heads // count
    groups = bands // pack
    rows = share * 64
    vmem = pl.BlockSpec(memory_space=pltpu.VMEM)
    hbm = pl.BlockSpec(memory_space=pl.ANY)
    smem = pl.BlockSpec(memory_space=pltpu.SMEM)
    sems = lambda n: pltpu.SemaphoreType.DMA((2, n))
    return pl.pallas_call(
        functools.partial(scan_kernel, views, pack, groups, share),
        in_specs=[smem] + [vmem] * 2 + [smem] + [vmem] * 3 + [hbm],
        out_specs=[vmem, hbm],
        out_shape=[
            jax.ShapeDtypeStruct((count, rows, 128), BF16),
            jax.ShapeDtypeStruct(x.shape, F32),
        ],
        scratch_shapes=[
            VMEM(x.shape, BF16),
            VMEM(x.shape, F32),
            pltpu.SemaphoreType.DMA,
            pltpu.SemaphoreType.DMA((3,)),
            VMEM((count, 8, 128), F32),
            VMEM((count, rows, 128), BF16),
            VMEM((count, 8, 128), F32),
            VMEM((rows, 128), BF16),
            VMEM((8, 128), F32),
            VMEM((groups, rows, 128), BF16),
            VMEM((groups, 8, 128), F32),
            VMEM((count + 1, rows, 128), F32),
            VMEM((count, 8, 128), F32),
            VMEM((count, rows, 128), BF16),
            sems(count), sems(count), sems(groups), sems(groups), sems(count),
        ],
        compiler_params=pltpu.CompilerParams(
            collective_id=0, has_side_effects=True, vmem_limit_bytes=VMEM_LIMIT
        ),
        name="scan_part",
    )(order, state.reshape(count, rows, 128), total, skip, col, row, score, x)


def token_kernel(
    bands, tile_ref, ent_ref, prefix_ref, col_ref, c_ref, gain_ref, inside_hbm, gate_hbm, w_hbm,
    out_ref,
    inside_s, gate_s, w_s, ecol_s, entry_s, normed_s, mine_s, got_s, load_sem, w_sem, sem,
):
    band, view = lax.axis_index("seq"), lax.axis_index("view")
    tokens, width = inside_s.shape
    width_out = w_s.shape[1]
    groups = tokens // GROUP
    pairs = width // 128
    piece = mine_s.shape[1]
    chunk = max(piece, TILE)
    chunks = tokens // chunk
    per_chunk = chunk // piece
    shift = (1 - band // (bands // 2)) * (chunks // 2)

    def chunk_of(i):
        return lax.rem(shift + i, chunks)

    def rows_of(i):
        return pl.ds(pl.multiple_of(chunk_of(i) * chunk, chunk), chunk)

    def loads(i):
        rows = rows_of(i)
        return (
            pltpu.make_async_copy(inside_hbm.at[rows], inside_s.at[rows], load_sem.at[0, i]),
            pltpu.make_async_copy(gate_hbm.at[rows], gate_s.at[rows], load_sem.at[1, i]),
        )

    load_w = pltpu.make_async_copy(w_hbm, w_s, w_sem)
    for copy in loads(0):
        copy.start()
    load_w.start()
    for i in range(1, chunks):
        for copy in loads(i):
            copy.start()

    barrier = pltpu.get_barrier_semaphore()

    def to(j):
        return {"seq": j, "view": view}

    for d in range(1, bands):
        pl.semaphore_signal(
            barrier, inc=1, device_id=to(lax.rem(band + d, bands)), device_id_type=MESH
        )

    ecol_s[...] = jnp.exp(col_ref[...])
    top_half = iota((128, 128), 0) < 64

    @pl.loop(0, pairs)
    def _(pair):
        rows = pl.ds(pl.multiple_of(pair * 128, 128), 128)
        mine = ent_ref[rows, :]
        entry_s[0, rows, :] = mine
        before = jnp.ones((128, 128), F32)
        for c in range(1, groups):
            e0, e1 = pair_columns(ecol_s[c * GROUP - 8 : c * GROUP, :], pair)
            before = before * jnp.where(top_half, e0[7:8, :], e1[7:8, :])
            entry = before * mine.astype(F32) + prefix_ref[c - 1, rows, :]
            entry_s[c, rows, :] = entry.astype(BF16)

    pl.semaphore_wait(barrier, bands - 1)

    def send(j):
        return pltpu.make_async_remote_copy(
            src_ref=mine_s.at[j], dst_ref=got_s.at[band],
            send_sem=sem.at[0, j], recv_sem=sem.at[1, band],
            device_id=to(j), device_id_type=MESH,
        )

    def arrival(i):
        return pltpu.make_async_remote_copy(
            src_ref=mine_s.at[i], dst_ref=got_s.at[i],
            send_sem=sem.at[0, i], recv_sem=sem.at[1, i],
            device_id=to(i), device_id_type=MESH,
        )

    first_half = iota((chunk, 128), 1) < 64
    same = (iota((128, 128), 0) < 64) == (iota((128, 128), 1) < 64)
    block = jnp.where(same, 1.0 / 64.0, 0.0).astype(BF16)
    for i in range(chunks):
        rows = rows_of(i)
        group = chunk_of(i) * chunk // GROUP
        for copy in loads(i):
            copy.wait()

        def one(pair):
            lanes = pl.ds(pl.multiple_of(pair * 128, 128), 128)
            e0, e1 = pair_columns(ecol_s[rows, :], pair)
            carried = nt(c_ref[rows, :], entry_s[group, lanes, :])
            carried = carried * jnp.where(first_half, e0, e1)
            gate = gate_s[rows, lanes].astype(F32)
            g = (inside_s[rows, lanes] + carried) * (gate / (1.0 + jnp.exp(-gate)))
            square = g * g
            high = square.astype(BF16)
            low = (square - high.astype(F32)).astype(BF16)
            mean = nn(high, block) + nn(low, block)
            normed = g * lax.rsqrt(mean + EPS) * gain_ref[:, lanes]
            normed_s[:, lanes] = normed.astype(BF16)

        @pl.loop(0, pairs // 4)
        def _(quad):
            for k in range(4):
                one(quad * 4 + k)

        if i == 0:
            load_w.wait()
        base = chunk_of(i) * per_chunk

        @pl.loop(0, width_out // 256)
        def _(n):
            cols = pl.ds(pl.multiple_of(n * 256, 256), 256)
            made = nn(normed_s[...], w_s[:, cols])
            for u in range(per_chunk):
                mine_s[base + u, :, cols] = made[u * piece : (u + 1) * piece, :].astype(BF16)

        for u in range(per_chunk):
            j = base + u

            @pl.when(j != band)
            def _(j=j):
                send(j).start()

    got_s[band] = mine_s[band]
    for d in range(1, bands):
        arrival(lax.rem(band - d + bands, bands)).wait_recv()
    for k in range(out_ref.shape[0]):
        per = out_ref.shape[1]
        tile = tile_ref[0, k]
        for u in range(per):
            out_ref[k, u] = got_s[tile * per + u]
    for d in range(1, bands):
        send(lax.rem(band + d, bands)).wait_send()


def token_part(tiles, ent, prefix, col, c, gain, inside, gate, w, bands):
    tokens, width = inside.shape
    width_out = w.shape[1]
    piece = tokens // bands
    chunk = max(piece, TILE)
    vmem = pl.BlockSpec(memory_space=pltpu.VMEM)
    hbm = pl.BlockSpec(memory_space=pl.ANY)
    return pl.pallas_call(
        functools.partial(token_kernel, bands),
        in_specs=[pl.BlockSpec(memory_space=pltpu.SMEM)] + [vmem] * 5 + [hbm] * 3,
        out_specs=vmem,
        out_shape=jax.ShapeDtypeStruct((tokens // TILE, TILE // piece, piece, width_out), BF16),
        scratch_shapes=[
            VMEM((tokens, width), F32),
            VMEM((tokens, width), BF16),
            VMEM(w.shape, BF16),
            VMEM((tokens, 128), F32),
            VMEM((tokens // GROUP, width, 128), BF16),
            VMEM((chunk, width), BF16),
            VMEM((bands, piece, width_out), BF16),
            VMEM((bands, piece, width_out), BF16),
            pltpu.SemaphoreType.DMA((2, tokens // chunk)),
            pltpu.SemaphoreType.DMA,
            pltpu.SemaphoreType.DMA((2, bands)),
        ],
        compiler_params=pltpu.CompilerParams(
            collective_id=1, has_side_effects=True, vmem_limit_bytes=VMEM_LIMIT
        ),
        name="token_part",
    )(tiles, ent, prefix, col, c, gain, inside, gate, w)


def shards(
    ssd_input, gate_input, b_matrix, c_matrix, log_decay,
    d_skip, norm_gain, out_weight, view_order, tile_order,
):
    views, bands = lax.axis_size("view"), lax.axis_size("seq")
    x, gate = ssd_input[0, 0], gate_input[0, 0]
    b, c, ld = b_matrix[0, 0], c_matrix[0, 0], log_decay[0, 0]
    tokens, width = x.shape
    state, prefix, col, row, score, total = local_part(x, b, c, ld)
    ent, inside = scan_part(view_order, state, total, col, row, score, d_skip, x, views, bands)
    out = token_part(
        tile_order, ent.reshape(width, 128), prefix, col, c, norm_gain[None, :],
        inside, gate, out_weight, bands,
    )
    return out.reshape(1, 1, tokens, out_weight.shape[1])


def solution(mesh):
    whole = P("seq", "view", None, None)
    in_specs = (whole,) * 5 + (P(), P(), P(), P("seq", None), P("seq", None))
    return jax.shard_map(
        shards, mesh=mesh, in_specs=in_specs, out_specs=whole, check_vma=False
    )
```

```python
import functools

import jax
import jax.numpy as jnp
from jax import lax
from jax.experimental import pallas as pl
from jax.experimental.pallas import tpu as pltpu
from jax.sharding import PartitionSpec as P

GROUP = 256
TILE = 128
EPS = 1e-05
MESH = pl.DeviceIdType.MESH
F32 = jnp.float32
BF16 = jnp.bfloat16
VMEM = pltpu.VMEM
VMEM_LIMIT = 64 * 1000 * 1000


def nn(a, b):
    return lax.dot_general(a, b, (((1,), (0,)), ((), ())), preferred_element_type=F32)


def nt(a, b):
    return lax.dot_general(a, b, (((1,), (1,)), ((), ())), preferred_element_type=F32)


def tn(a, b):
    return lax.dot_general(a, b, (((0,), (0,)), ((), ())), preferred_element_type=F32)


def split3(a):
    hi = a.astype(BF16)
    rest = a - hi.astype(F32)
    mid = rest.astype(BF16)
    low = (rest - mid.astype(F32)).astype(BF16)
    return hi, mid, low


def iota(shape, dim):
    return lax.broadcasted_iota(jnp.int32, shape, dim)


def pair_columns(full, pair):
    lanes = full.shape[1]
    turned = pltpu.roll(full, lax.rem(lanes - 2 * pair, lanes), 1)
    return turned[:, 0:1], turned[:, 1:2]


def mixer_kernel(
    views, pack, groups, share, bands,
    order_ref, skip_ref, b_ref, c_ref, ld_ref, gain_ref, x_hbm, gate_hbm, w_hbm,
    out_hbm,
    x_s, inside_s, gate_s, w_s, sem_x, sem_g, sem_w, sem_o,
    col_ref, row_ref, score_ref, scale_s, total_s, state_ref, prefix_ref, ent_s,
    note_s, got_s, gotnote_s, agg_s, aggnote_s, aggs_s, aggnotes_s, within_s, before_s, send_s,
    sem_a, sem_an, sem_b, sem_bn, sem_c,
    ecol_s, entry_s, normed_s, mine_s, sem,
):
    band, view = lax.axis_index("seq"), lax.axis_index("view")
    count = views * pack
    group, member = band // pack, lax.rem(band, pack)
    me = member * views + view
    rows = share * 64
    heads, tokens = ld_ref.shape
    spans = tokens // GROUP
    pairs = x_s.shape[1] // 128
    first_half = iota((GROUP, 128), 1) < 64
    top_half = iota((128, 128), 0) < 64

    load = pltpu.make_async_copy(x_hbm, x_s, sem_x)
    load_gate = pltpu.make_async_copy(gate_hbm, gate_s, sem_g)
    load_w = pltpu.make_async_copy(w_hbm, w_s, sem_w)
    load.start()
    load_gate.start()
    load_w.start()

    barrier = pltpu.get_barrier_semaphore()
    for d in range(1, bands):
        pl.semaphore_signal(
            barrier, inc=1,
            device_id={"seq": lax.rem(band + d, bands), "view": view}, device_id_type=MESH,
        )
    for d in range(1, views):
        for m in range(pack):
            pl.semaphore_signal(
                barrier, inc=1,
                device_id={"seq": group * pack + m, "view": lax.rem(view + d, views)},
                device_id_type=MESH,
            )

    at_row, at_col = iota((GROUP, GROUP), 0), iota((GROUP, GROUP), 1)
    lower = jnp.where(at_col <= at_row, 1.0, 0.0).astype(BF16)
    upper = jnp.where(at_row <= at_col, 1.0, 0.0).astype(BF16)
    total = jnp.zeros((heads, 1), F32)
    for c in range(spans):
        span = slice(c * GROUP, (c + 1) * GROUP)
        own = ld_ref[:, span]
        padded = jnp.concatenate([own, jnp.zeros((128 - heads, GROUP), F32)], axis=0)
        lines = sum(nn(part, upper) for part in split3(own))
        row_ref[:, span] = lines
        cols = sum(nt(lower, part) for part in split3(padded))
        col_ref[span, :] = cols
        ecol_s[span, :] = jnp.exp(cols)
        scale_s[span, :] = jnp.exp(jnp.minimum(cols[GROUP - 1 : GROUP, :] - cols, 0.0))
        total = total + lines[:, GROUP - 1 : GROUP]
        scores = nt(c_ref[span, :], b_ref[span, :])
        score_ref[c] = jnp.where(at_col <= at_row, scores, 0.0)
    total_s[...] = jnp.broadcast_to(total, total_s.shape)

    rank = jnp.int32(0)
    for r in range(views):
        rank = rank + jnp.where(order_ref[0, r] == view, r, 0)
    key = (rank + member * views).astype(F32)
    for q in range(count):
        note_s[q, 0:share, :] = total_s[q * share : (q + 1) * share, :]
        note_s[q, share : share + 1, :] = jnp.full((1, 128), key, F32)

    def states_of(q):
        for j in range(share // 2):
            pair = q * (share // 2) + j
            at = slice(j * 128, (j + 1) * 128)
            lanes = pl.ds(pl.multiple_of(pair * 128, 128), 128)
            f0, f1 = pair_columns(scale_s[...], pair)
            running = jnp.zeros((128, 128), F32)
            for c in range(spans):
                span = slice(c * GROUP, (c + 1) * GROUP)
                bf = b_ref[span, :].astype(F32)
                scaled = jnp.concatenate(
                    [(f0[span, :] * bf).astype(BF16), (f1[span, :] * bf).astype(BF16)], axis=1
                )
                both = tn(x_s[span, lanes], scaled)
                state = jnp.where(top_half, both[:, 0:128], both[:, 128:256])
                if c:
                    prefix_ref[c - 1, lanes, :] = running
                e0 = row_ref[pl.ds(2 * pair, 1), span][:, GROUP - 1 : GROUP]
                e1 = row_ref[pl.ds(2 * pair + 1, 1), span][:, GROUP - 1 : GROUP]
                running = jnp.exp(jnp.where(top_half, e0, e1)) * running + state
            state_ref[q, at, :] = running.astype(BF16)

    cuts = [0, pairs * 3 // 8, pairs * 11 // 16, pairs]
    def inside_span(part):
        @pl.loop(cuts[part], cuts[part + 1])
        def _(pair):
            cols = pair_columns(col_ref[...], pair)
            lanes = pl.ds(pl.multiple_of(pair * 128, 128), 128)
            for c in range(x_s.shape[0] // GROUP):
                span = slice(c * GROUP, (c + 1) * GROUP)
                x = x_s[span, lanes]
                outs = []
                for j, col in enumerate(cols):
                    line = row_ref[pl.ds(2 * pair + j, 1), span]
                    gap = jnp.minimum(col[span, :] - line, 0.0)
                    outs.append(nn((jnp.exp(gap) * score_ref[c]).astype(BF16), x))
                inside_s[span, lanes] = (
                    jnp.where(first_half, outs[0], outs[1])
                    + jnp.where(first_half, skip_ref[2 * pair], skip_ref[2 * pair + 1]) * x.astype(F32)
                )

    def peer(q):
        return {"seq": group * pack + q // views, "view": lax.rem(q, views)}

    def across(g):
        return {"seq": g * pack + member, "view": view}

    def exchange(source, target, sem, d, q):
        return pltpu.make_async_remote_copy(
            src_ref=source, dst_ref=target, send_sem=sem.at[0, d], recv_sem=sem.at[1, d],
            device_id=peer(q), device_id_type=MESH,
        )

    sends = []
    load.wait()
    pl.semaphore_wait(barrier, bands - 1 + (views - 1) * pack)
    for d in range(1, count):
        q = lax.rem(me + d, count)
        sends.append(exchange(note_s.at[q], gotnote_s.at[me], sem_an, d, q))
        sends[-1].start()
        states_of(q)
        sends.append(exchange(state_ref.at[q], got_s.at[me], sem_a, d, q))
        sends[-1].start()
    states_of(me)
    got_s[me] = state_ref[me]
    gotnote_s[me] = note_s[me]
    inside_span(0)
    for d in range(1, count):
        src = lax.rem(me - d + count, count)
        exchange(note_s.at[src], gotnote_s.at[src], sem_an, d, src).wait_recv()
        exchange(state_ref.at[src], got_s.at[src], sem_a, d, src).wait_recv()

    logs = [gotnote_s[b] for b in range(count)]
    keys = [jnp.broadcast_to(log[share : share + 1, :], log.shape) for log in logs]
    zero = jnp.zeros_like(logs[0])
    before, upto, whole = [], [], zero
    for b in range(count):
        acc = zero
        for o in range(count):
            if o != b:
                acc = acc + jnp.where(keys[o] < keys[b], logs[o], 0.0)
        before.append(acc)
        upto.append(acc + logs[b])
        before_s[b] = jnp.exp(acc)
        whole = whole + logs[b]
    aggnote_s[...] = whole
    last = [jnp.exp(jnp.minimum(whole - upto[b], 0.0)) for b in range(count)]
    for i in range(share):
        span = slice(i * 64, (i + 1) * 64)
        acc = jnp.zeros((64, 128), F32)
        for b in range(count):
            acc = acc + last[b][i : i + 1, :] * got_s[b, span, :].astype(F32)
        agg_s[span, :] = acc.astype(BF16)

    def ahead(source, target, sem, k, g):
        return pltpu.make_async_remote_copy(
            src_ref=source, dst_ref=target, send_sem=sem.at[0, k], recv_sem=sem.at[1, k],
            device_id=across(g), device_id_type=MESH,
        )

    def ahead_pair(k, g):
        return (
            ahead(aggnote_s, aggnotes_s.at[k], sem_bn, k, g),
            ahead(agg_s, aggs_s.at[k], sem_b, k, g),
        )

    for k in range(groups - 1, 0, -1):
        @pl.when(group + k < groups)
        def _(k=k):
            for copy in ahead_pair(k, group + k):
                copy.start()

    for b in range(count):
        coefs = [
            jnp.where(
                keys[o] < keys[b], jnp.exp(jnp.minimum(before[b] - upto[o], 0.0)), 0.0
            )
            for o in range(count)
            if o != b
        ]
        others = [o for o in range(count) if o != b]
        for i in range(share):
            span = slice(i * 64, (i + 1) * 64)
            acc = jnp.zeros((64, 128), F32)
            for o, coef in zip(others, coefs):
                acc = acc + coef[i : i + 1, :] * got_s[o, span, :].astype(F32)
            within_s[b, span, :] = acc

    inside_span(1)
    carry = within_s.at[count]
    carry[...] = jnp.zeros((rows, 128), F32)
    for k in range(groups - 1, 0, -1):
        @pl.when(group - k >= 0)
        def _(k=k):
            for copy in ahead_pair(k, group - k):
                copy.wait_recv()
            decay = jnp.exp(aggnotes_s[k])
            for i in range(share):
                span = slice(i * 64, (i + 1) * 64)
                carry[span, :] = decay[i : i + 1, :] * carry[span, :] + aggs_s[k, span, :].astype(F32)

    def entering(q):
        factor = before_s[q]
        parts = []
        for i in range(share):
            span = slice(i * 64, (i + 1) * 64)
            parts.append(factor[i : i + 1, :] * carry[span, :] + within_s[q, span, :])
        return jnp.concatenate(parts, axis=0).astype(BF16)

    for d in range(1, count):
        q = lax.rem(me + d, count)
        send_s[d] = entering(q)
        sends.append(exchange(send_s.at[d], ent_s.at[me], sem_c, d, q))
        sends[-1].start()
    ent_s[me] = entering(me)
    inside_span(2)
    for d in range(1, count):
        src = lax.rem(me - d + count, count)
        exchange(send_s.at[d], ent_s.at[src], sem_c, d, src).wait_recv()
    tokens, width = inside_s.shape
    width_out = w_s.shape[1]
    piece = mine_s.shape[1]
    chunk = max(piece, TILE)
    chunks = tokens // chunk
    per_chunk = chunk // piece
    shift = (1 - band // (bands // 2)) * (chunks // 2)

    def chunk_of(i):
        return lax.rem(shift + i, chunks)

    def rows_of(i):
        return pl.ds(pl.multiple_of(chunk_of(i) * chunk, chunk), chunk)

    def to(j):
        return {"seq": j, "view": view}

    @pl.loop(0, pairs)
    def _(pair):
        rows = pl.ds(pl.multiple_of(pair * 128, 128), 128)
        per = share // 2
        mine = ent_s[pair // per, pl.ds(pl.multiple_of(lax.rem(pair, per) * 128, 128), 128), :]
        entry_s[0, rows, :] = mine
        before = jnp.ones((128, 128), F32)
        for c in range(1, spans):
            e0, e1 = pair_columns(ecol_s[c * GROUP - 8 : c * GROUP, :], pair)
            before = before * jnp.where(top_half, e0[7:8, :], e1[7:8, :])
            entry = before * mine.astype(F32) + prefix_ref[c - 1, rows, :]
            entry_s[c, rows, :] = entry.astype(BF16)

    load_gate.wait()
    def send(j):
        return pltpu.make_async_remote_copy(
            src_ref=mine_s.at[j], dst_ref=out_hbm.at[band],
            send_sem=sem.at[0, j], recv_sem=sem.at[1, band],
            device_id=to(j), device_id_type=MESH,
        )

    def arrival(i):
        return pltpu.make_async_remote_copy(
            src_ref=mine_s.at[i], dst_ref=out_hbm.at[i],
            send_sem=sem.at[0, i], recv_sem=sem.at[1, i],
            device_id=to(i), device_id_type=MESH,
        )

    half = iota((chunk, 128), 1) < 64
    same = (iota((128, 128), 0) < 64) == (iota((128, 128), 1) < 64)
    block = jnp.where(same, 1.0 / 64.0, 0.0).astype(BF16)
    for i in range(chunks):
        rows = rows_of(i)
        part = chunk_of(i) * chunk // GROUP
        def one(pair):
            lanes = pl.ds(pl.multiple_of(pair * 128, 128), 128)
            e0, e1 = pair_columns(ecol_s[rows, :], pair)
            carried = nt(c_ref[rows, :], entry_s[part, lanes, :])
            carried = carried * jnp.where(half, e0, e1)
            gate = gate_s[rows, lanes].astype(F32)
            g = (inside_s[rows, lanes] + carried) * (gate / (1.0 + jnp.exp(-gate)))
            square = g * g
            high = square.astype(BF16)
            low = (square - high.astype(F32)).astype(BF16)
            mean = nn(high, block) + nn(low, block)
            normed = g * lax.rsqrt(mean + EPS) * gain_ref[:, lanes]
            normed_s[:, lanes] = normed.astype(BF16)

        @pl.loop(0, pairs // 4)
        def _(quad):
            for k in range(4):
                one(quad * 4 + k)

        if i == 0:
            load_w.wait()
        base = chunk_of(i) * per_chunk

        @pl.loop(0, width_out // 256)
        def _(n):
            cols = pl.ds(pl.multiple_of(n * 256, 256), 256)
            made = nn(normed_s[...], w_s[:, cols])
            for u in range(per_chunk):
                mine_s[base + u, :, cols] = made[u * piece : (u + 1) * piece, :].astype(BF16)

        for u in range(per_chunk):
            j = base + u

            @pl.when(j != band)
            def _(j=j):
                send(j).start()

    keep = pltpu.make_async_copy(mine_s.at[band], out_hbm.at[band], sem_o)
    keep.start()
    for d in range(1, bands):
        arrival(lax.rem(band - d + bands, bands)).wait_recv()
    for copy in sends:
        copy.wait_send()
    for step in range(1, groups):
        @pl.when(group + step < groups)
        def _(step=step):
            for copy in ahead_pair(step, group + step):
                copy.wait_send()
    for d in range(1, bands):
        send(lax.rem(band + d, bands)).wait_send()
    keep.wait()


def mixer_part(order, skip, b, c, ld, gain, x, gate, w, views, bands):
    heads, tokens = ld.shape
    width, width_out = w.shape
    pack = 2 if bands % 2 == 0 and heads % (4 * views) == 0 else 1
    count = views * pack
    share = heads // count
    groups = bands // pack
    rows = share * 64
    piece = tokens // bands
    spans = tokens // GROUP
    vmem = pl.BlockSpec(memory_space=pltpu.VMEM)
    hbm = pl.BlockSpec(memory_space=pl.ANY)
    smem = pl.BlockSpec(memory_space=pltpu.SMEM)
    dma = pltpu.SemaphoreType.DMA
    sems = lambda n: dma((2, n))
    return pl.pallas_call(
        functools.partial(mixer_kernel, views, pack, groups, share, bands),
        in_specs=[smem] * 2 + [vmem] * 4 + [hbm] * 3,
        out_specs=hbm,
        out_shape=jax.ShapeDtypeStruct((bands, piece, width_out), BF16),
        scratch_shapes=[
            VMEM(x.shape, BF16),
            VMEM(x.shape, F32),
            VMEM(x.shape, BF16),
            VMEM(w.shape, BF16),
            dma, dma, dma, dma,
            VMEM((tokens, 128), F32),
            VMEM((heads, tokens), F32),
            VMEM((spans, GROUP, GROUP), F32),
            VMEM((tokens, 128), F32),
            VMEM((heads, 128), F32),
            VMEM((count, rows, 128), BF16),
            VMEM((spans - 1, width, 128), F32),
            VMEM((count, rows, 128), BF16),
            VMEM((count, 8, 128), F32),
            VMEM((count, rows, 128), BF16),
            VMEM((count, 8, 128), F32),
            VMEM((rows, 128), BF16),
            VMEM((8, 128), F32),
            VMEM((groups, rows, 128), BF16),
            VMEM((groups, 8, 128), F32),
            VMEM((count + 1, rows, 128), F32),
            VMEM((count, 8, 128), F32),
            VMEM((count, rows, 128), BF16),
            sems(count), sems(count), sems(groups), sems(groups), sems(count),
            VMEM((tokens, 128), F32),
            VMEM((spans, width, 128), BF16),
            VMEM((max(piece, TILE), width), BF16),
            VMEM((bands, piece, width_out), BF16),
            sems(bands),
        ],
        compiler_params=pltpu.CompilerParams(
            collective_id=0, has_side_effects=True, vmem_limit_bytes=VMEM_LIMIT
        ),
        name="mixer_part",
    )(order, skip, b, c, ld, gain, x, gate, w)


def tile_kernel(order_ref, in_ref, out_ref):
    out_ref[...] = in_ref[...]


def tile_part(order, pieces):
    bands, piece, width = pieces.shape
    per = TILE // piece
    block = (per, piece, width)
    return pl.pallas_call(
        tile_kernel,
        grid_spec=pltpu.PrefetchScalarGridSpec(
            num_scalar_prefetch=1,
            grid=(bands // per,),
            in_specs=[pl.BlockSpec(block, lambda k, order: (order[k], 0, 0))],
            out_specs=pl.BlockSpec(block, lambda k, order: (k, 0, 0)),
        ),
        out_shape=jax.ShapeDtypeStruct(pieces.shape, BF16),
        compiler_params=pltpu.CompilerParams(vmem_limit_bytes=VMEM_LIMIT),
        name="tile_part",
    )(order, pieces)


def shards(
    ssd_input, gate_input, b_matrix, c_matrix, log_decay,
    d_skip, norm_gain, out_weight, view_order, tile_order,
):
    views, bands = lax.axis_size("view"), lax.axis_size("seq")
    x, gate = ssd_input[0, 0], gate_input[0, 0]
    b, c, ld = b_matrix[0, 0], c_matrix[0, 0], log_decay[0, 0]
    tokens, width = x.shape
    pieces = mixer_part(
        view_order, d_skip, b, c, ld, norm_gain[None, :], x, gate, out_weight, views, bands
    )
    out = tile_part(tile_order[0], pieces)
    return out.reshape(1, 1, tokens, out_weight.shape[1])


def solution(mesh):
    whole = P("seq", "view", None, None)
    in_specs = (whole,) * 5 + (P(), P(), P(), P("seq", None), P("seq", None))
    return jax.shard_map(
        shards, mesh=mesh, in_specs=in_specs, out_specs=whole, check_vma=False
    )
```
